32 devices in a mesh: groups: 2 (over x), cache: 16 (over z, y, core).
Axes of the slice: x: 2, y: 2, z: 4, core: 2. Of those that a mesh axis runs over, the one named last changes fastest.
Arguments:
- prefix_len: int32 [32], P('groups'), parts along dimension 0, may hold values from 128 to 1024, as said below
- hits: int32 [32, 1], P('groups'), parts along dimension 0, may hold values from 0 to 15, as said below
- span_block: int32 [32, 16], P('groups'), parts along dimension 0, may hold values from 0 to 15, each once within a row
- queries: bfloat16 [2048, 2048], P(('groups', 'cache')), parts along dimension 0, may hold values from -100 to 100
- fresh_keys: bfloat16 [2048, 128], P(('groups', 'cache')), parts along dimension 0, may hold values from -4 to 4
- fresh_values: bfloat16 [2048, 128], P(('groups', 'cache')), parts along dimension 0, may hold values from -4 to 4
- cache_keys: bfloat16 [65536, 128], P(('groups', 'cache')), parts along dimension 0, may hold values from -4 to 4
- cache_values: bfloat16 [65536, 128], P(('groups', 'cache')), parts along dimension 0, may hold values from -4 to 4
Outputs:
- attended: bfloat16 [2048, 2048], P(('groups', 'cache')), parts along dimension 0
The draws below stay inside these ranges and needn't reach their ends.
There are 2 independent parts, one for each index of `groups`. The reference program is written for one: setup_inputs(seed, part) draws one part's arguments, and reference() takes and returns one part's arrays. A program takes and returns all parts, laid end to end along the dimension named above; each array names one. Nothing has to cross between parts.
Inputs may be any that keep to these rules, and one draw needn't show every extreme that they name: `prefix_len`: every request's prefix holds at least 128 tokens, and one request in every draw holds exactly 1024. `hits`: each row names 1 different devices. Each device is named by at most 2 requests; 4 devices are named by exactly 2, half of them by one, a quarter by none. `span_block`: each row is a permutation.
All inputs are finite; a program needn't handle non-finite values.
Results may differ from the reference program's by a relative error of at most 0.0065.
Values may be sent and summed in bfloat16 or wider, within the bound.
A program may use at most 64 MiB of HBM per device.

```python
import jax
import jax.numpy as jnp
from jax import lax

HEADS = 16
HD = 128
PAGE = 128
CAP = 2
REQUESTS = 16
TOK_REQ = 4
PAGES_DEV = 16
HITS = 1
TOKENS = 1024
CACHE_ROWS = 32768
PREFIX = 1024
N_CACHE = 16


def hit_table(key):
    seeded = jax.random.fold_in(key, 101)
    shuffled = jax.random.permutation(jax.random.fold_in(seeded, 1), N_CACHE)
    doubled = N_CACHE // 4
    listing = jnp.concatenate([shuffled[:N_CACHE - doubled], shuffled[:doubled]]).reshape(REQUESTS, HITS)
    row_order = jax.random.permutation(jax.random.fold_in(seeded, 2), REQUESTS)
    listing = jnp.take(listing, row_order, axis=0)
    row_keys = jax.random.split(jax.random.fold_in(seeded, 3), REQUESTS)

    def one_order(row_key):
        return jax.random.permutation(row_key, HITS)
    col_order = jax.vmap(one_order)(row_keys)
    return jnp.take_along_axis(listing, col_order, axis=1).astype(jnp.int32)


def paired_table(key, count, salt):
    drawn_values = jax.random.normal(jax.random.fold_in(key, salt + 2), (count, HD), jnp.float32)
    return jnp.clip(drawn_values, -4.0, 4.0)


def draw_prefix_len(key, part):
    lengths = jax.random.randint(jax.random.fold_in(key, 202), (REQUESTS,), PREFIX // 8, PREFIX + 1)
    longest = jax.random.randint(jax.random.fold_in(key, 203), (), 0, REQUESTS)
    return lengths.at[longest].set(PREFIX).astype(jnp.int32)


def draw_hits(key, part):
    return hit_table(key)


def draw_fresh_keys(key, part):
    return paired_table(key, TOKENS, 301).astype(jnp.bfloat16)


def draw_cache_keys(key, part):
    return paired_table(key, CACHE_ROWS, 311).astype(jnp.bfloat16)


def draw_queries(key, part):
    drawn_values = jnp.clip(jax.random.normal(jax.random.fold_in(key, 402), (TOKENS, HEADS, HD), jnp.float32), -4.0, 4.0)
    return drawn_values.reshape(TOKENS, HEADS * HD).astype(jnp.bfloat16)


def level_of(stream_key, shape, cuts, low, top_value):
    loudness, own = 1.0, jax.random.fold_in(stream_key, 6)
    for axis_at, blocks in cuts:
        steps = jnp.exp(jax.random.uniform(jax.random.fold_in(own, axis_at), (blocks,), jnp.float32, low / len(cuts), top_value / len(cuts)))
        loudness = loudness * jnp.repeat(steps, shape[axis_at] // blocks).reshape([-1 if axis == axis_at else 1 for axis in range(len(shape))])
    return loudness


def normal_values(key, shape, scale, most, pieces=(), held_as=jnp.bfloat16):
    values = scale * jax.random.normal(key, shape, jnp.float32)
    if pieces:
        values = values * level_of(key, shape, pieces, -0.22, 0.18)
    return jnp.clip(values, -most, most).astype(held_as)


def setup_inputs(seed: int = 0, part: int = 0) -> dict:
    keys = jax.random.split(jax.random.key(seed), 9)
    part_keys = jax.random.split(jax.random.fold_in(keys[8], part), 9)
    prefix_len = draw_prefix_len(jax.random.fold_in(jax.random.fold_in(keys[8], part), 71), part)
    hits = draw_hits(jax.random.fold_in(jax.random.fold_in(keys[8], part), 71), part)
    span_block = jax.vmap(lambda own: jax.random.permutation(own, N_CACHE))(jax.random.split(part_keys[2], REQUESTS)).reshape((REQUESTS, N_CACHE)).astype(jnp.int32)
    queries = draw_queries(jax.random.fold_in(jax.random.fold_in(keys[8], part), 71), part)
    fresh_keys = draw_fresh_keys(jax.random.fold_in(jax.random.fold_in(keys[8], part), 71), part)
    fresh_values = normal_values(part_keys[5], (TOKENS, HD), 1.0, 4.0, ((0, 16),))
    cache_keys = draw_cache_keys(jax.random.fold_in(jax.random.fold_in(keys[8], part), 71), part)
    cache_values = normal_values(part_keys[7], (CACHE_ROWS, HD), 1.0, 4.0, ((0, 16),))
    return {"prefix_len": prefix_len, "hits": hits, "span_block": span_block, "queries": queries, "fresh_keys": fresh_keys, "fresh_values": fresh_values, "cache_keys": cache_keys, "cache_values": cache_values}


floor_score = -1e30


def attend(query_rows, key_rows, value_rows, visible, rounding):
    scale = HD ** -0.5
    scores = jnp.einsum("qhd,kd->qhk", query_rows, key_rows, precision=lax.Precision.HIGHEST) * scale
    scores = jnp.where(visible[:, None, :], scores, floor_score)
    maxima = jnp.max(scores, axis=2)
    weights = jnp.exp(scores - maxima[:, :, None]) * visible[:, None, :]
    totals = jnp.sum(weights, axis=2)
    if rounding:
        weights = lax.optimization_barrier(weights.astype(jnp.bfloat16)).astype(jnp.float32)
    summed = jnp.einsum("qhk,kd->qhd", weights, value_rows, precision=lax.Precision.HIGHEST)
    return maxima, totals, summed


def reference(prefix_len, hits, span_block, queries, fresh_keys, fresh_values, cache_keys, cache_values):
    region = (PAGES_DEV // CAP) * PAGE
    per_device = REQUESTS * TOK_REQ
    matches = jnp.any(hits[:, :, None, None] == hits[None, None, :, :], axis=3)
    earlier = jnp.arange(REQUESTS)[None, None, :] < jnp.arange(REQUESTS)[:, None, None]
    slot_rank = jnp.sum(matches & earlier, axis=2).astype(jnp.int32)
    offsets = jnp.arange(TOK_REQ, dtype=jnp.int32)
    devices = jnp.arange(N_CACHE, dtype=jnp.int32)
    spots = jnp.arange(region, dtype=jnp.int32)

    def one_request(request):
        row_index = (devices[:, None] * per_device + request * TOK_REQ + offsets[None, :]).reshape(-1).astype(jnp.int32)
        query_rows = jnp.take(queries, row_index, axis=0).astype(jnp.float32).reshape(-1, HEADS, HD)
        key_rows = jnp.take(fresh_keys, row_index, axis=0).astype(jnp.float32)
        value_rows = jnp.take(fresh_values, row_index, axis=0).astype(jnp.float32)
        positions = (span_block[request][:, None] * TOK_REQ + offsets[None, :]).reshape(-1)
        causal = positions[None, :] <= positions[:, None]
        maxima, totals, summed = attend(query_rows, key_rows, value_rows, causal, False)
        prompt_out = summed / totals[:, :, None]
        prompt_lse = maxima + jnp.log(totals)

        def one_owner(which):
            owner = hits[request, which]
            start = (owner * PAGES_DEV * PAGE + slot_rank[request, which] * region).astype(jnp.int32)
            page_keys = lax.dynamic_slice_in_dim(cache_keys, start, region, 0).astype(jnp.float32)
            page_values = lax.dynamic_slice_in_dim(cache_values, start, region, 0).astype(jnp.float32)
            visible = ((which * region + spots) < prefix_len[request])[None, :]
            owner_max, owner_total, owner_sum = attend(query_rows, page_keys, page_values, visible, True)
            owner_total = jnp.maximum(owner_total, 1.0)
            owner_out = (owner_sum / owner_total[:, :, None]).astype(jnp.bfloat16)
            return owner_out, owner_max + jnp.log(owner_total)

        owner_out, owner_lse = lax.map(one_owner, jnp.arange(HITS, dtype=jnp.int32))
        owner_wide = lax.optimization_barrier(owner_out).astype(jnp.float32)
        every_lse = jnp.concatenate([prompt_lse[None], owner_lse], axis=0)
        highest = jnp.max(every_lse, axis=0)
        shares = jnp.exp(every_lse - highest[None])
        combined = shares[0][:, :, None] * prompt_out + jnp.sum(shares[1:][:, :, :, None] * owner_wide, axis=0)
        result = combined / jnp.sum(shares, axis=0)[:, :, None]
        return result.astype(jnp.bfloat16).reshape(N_CACHE, TOK_REQ, HEADS * HD)

    blocks = lax.map(one_request, jnp.arange(REQUESTS, dtype=jnp.int32))
    return jnp.transpose(blocks, (1, 0, 2, 3)).reshape(N_CACHE * per_device, HEADS * HD)
```

```python
import functools
import math

import jax
import jax.numpy as jnp
from jax import lax
from jax.experimental import pallas as pl
from jax.experimental.pallas import tpu as pltpu
from jax.sharding import PartitionSpec as P

HEADS = 16
HD = 128
PAGE = 128
CAP = 2
REQUESTS = 16
TOK = 4
PAGES_DEV = 16
REGION = PAGES_DEV // CAP * PAGE
PER_DEV = REQUESTS * TOK
PLANE = 4
ROWS = PLANE * TOK * HEADS
MESH = pl.DeviceIdType.MESH
FLOOR = -1e30
EXP2_SCALE = HD**-0.5 * math.log2(math.e)


def flip(a, b, size):
    out, bit = 0, 1
    while bit < size:
        out = out + ((a // bit + b // bit) % 2) * bit
        bit *= 2
    return out


def attend(q, k, v, visible):
    s = lax.dot_general(q, k, (((1,), (1,)), ((), ())), preferred_element_type=jnp.float32)
    s = jnp.where(visible, s, FLOOR)
    m = jnp.max(s, axis=1, keepdims=True)
    p = jnp.exp2((s - m) * EXP2_SCALE).astype(jnp.bfloat16)
    v1 = jnp.concatenate([v, jnp.ones_like(v)], axis=1)
    o = jnp.dot(p, v1, preferred_element_type=jnp.float32)
    return m, o


def head_lanes(x, units):
    x = x.reshape(units, HEADS, HD)
    head = lax.broadcasted_iota(jnp.int32, (units, HEADS, HD), 1)
    lane = lax.broadcasted_iota(jnp.int32, (units, HEADS, HD), 2)
    return jnp.sum(jnp.where(head == lane, x, 0.0), axis=1)


def head_rows(x, units):
    head = lax.broadcasted_iota(jnp.int32, (units, HEADS, HD), 1)
    lane = lax.broadcasted_iota(jnp.int32, (units, HEADS, HD), 2)
    wide = jnp.broadcast_to(x[:, None, :], (units, HEADS, HD))
    return jnp.sum(jnp.where(head == lane, wide, 0.0), axis=2, keepdims=True)


def kernel(n, hit_count, dims, prefix, hits, span, qx, fk, fv, ck, cv, out,
           send, arrived, ret, back, lret, lback, kv, kc, vc, pout, plse, comb, lcomb,
           qs, qr, rs, rr, ls, lr, s1s, s1r, s2s, s2r, s3s, s3r, loc):
    me = lax.axis_index("cache")
    zs, ys = dims
    planes = n // PLANE
    core = me % 2
    y = (me // 2) % ys
    z = me // (2 * ys)
    my_plane = me // PLANE

    loads = [
        pltpu.make_async_copy(fk, kv.at[z, y, core, 0], loc.at[0]),
        pltpu.make_async_copy(fv, kv.at[z, y, core, 1], loc.at[1]),
        pltpu.make_async_copy(ck, kc, loc.at[2]),
        pltpu.make_async_copy(cv, vc, loc.at[3]),
    ]
    for load in loads:
        load.start()

    barrier = pltpu.get_barrier_semaphore()

    @pl.loop(1, n)
    def _(k):
        pl.semaphore_signal(barrier, inc=1, device_id={"cache": (me + k) % n}, device_id_type=MESH)

    def named_by(d):
        first = jnp.int32(REQUESTS - 1)
        last = jnp.int32(0)
        for r in range(REQUESTS):
            for i in range(hit_count):
                here = hits[r, i] == d
                first = jnp.where(here, jnp.minimum(first, r), first)
                last = jnp.where(here, r, last)
        return first, last

    @pl.loop(0, n)
    def _(d):
        first, last = named_by(d)
        send[d, 0] = qx[first]
        send[d, 1] = qx[last]

    pl.semaphore_wait(barrier, n - 1)
    loads[0].wait()
    loads[1].wait()

    def kv1(dz, at_z):
        return pltpu.make_async_remote_copy(
            src_ref=kv.at[at_z, y, core], dst_ref=kv.at[at_z, y, core],
            send_sem=s1s.at[dz], recv_sem=s1r.at[dz],
            device_id={"cache": (((z + dz) % zs) * ys + y) * 2 + core}, device_id_type=MESH)

    def kv2(dy, at_y):
        return pltpu.make_async_remote_copy(
            src_ref=kv.at[:, at_y, core], dst_ref=kv.at[:, at_y, core],
            send_sem=s2s.at[dy], recv_sem=s2r.at[dy],
            device_id={"cache": (z * ys + (y + dy) % ys) * 2 + core}, device_id_type=MESH)

    def kv3(at_core):
        return pltpu.make_async_remote_copy(
            src_ref=kv.at[:, :, at_core], dst_ref=kv.at[:, :, at_core],
            send_sem=s3s.at[0], recv_sem=s3r.at[0],
            device_id={"cache": (z * ys + y) * 2 + 1 - core}, device_id_type=MESH)

    for dz in range(1, zs):
        kv1(dz, z).start()

    def query_copy(to, frm):
        return pltpu.make_async_remote_copy(
            src_ref=send.at[to], dst_ref=arrived.at[frm], send_sem=qs.at[to], recv_sem=qr.at[frm],
            device_id={"cache": to}, device_id_type=MESH)

    def out_copy(to, frm):
        return pltpu.make_async_remote_copy(
            src_ref=ret.at[to], dst_ref=back.at[frm], send_sem=rs.at[to], recv_sem=rr.at[frm],
            device_id={"cache": to}, device_id_type=MESH)

    def lse_copy(to, frm):
        return pltpu.make_async_remote_copy(
            src_ref=lret.at[to], dst_ref=lback.at[frm], send_sem=ls.at[to], recv_sem=lr.at[frm],
            device_id={"cache": to}, device_id_type=MESH)

    def peers(j, act):
        base = flip(my_plane, j, planes) * PLANE

        @pl.loop(0, PLANE)
        def _(k):
            d = base + (me + k) % PLANE

            @pl.when(d != me)
            def _():
                act(d)

    @pl.loop(0, planes)
    def _(i):
        peers((planes // 2 + i) % planes, lambda d: query_copy(d, me).start())

    arrived[me] = send[me]
    loads[2].wait()
    loads[3].wait()

    limits = []
    for request in named_by(me):
        place = jnp.int32(0)
        for i in range(hit_count):
            place = jnp.where(hits[request, i] == me, i, place)
        limits.append(prefix[request] - place * REGION)
    spot = lax.broadcasted_iota(jnp.int32, (1, REGION), 1)

    def serve(j):
        peers(j, lambda d: query_copy(d, d).wait_recv())
        base = flip(my_plane, j, planes) * PLANE

        for slot in range(CAP):
            q = arrived[pl.ds(base, PLANE), slot].reshape(ROWS, HD)
            part = pl.ds(slot * REGION, REGION)
            m, o = attend(q, kc[part], vc[part], spot < limits[slot])
            total = jnp.maximum(o[:, HD:], 1.0)
            lse = m * EXP2_SCALE + jnp.log2(total)
            lse = jnp.where(limits[slot] > 0, lse, FLOOR)
            result = (o[:, :HD] / total).astype(jnp.bfloat16)
            ret[pl.ds(base, PLANE), slot] = result.reshape(PLANE, TOK, HEADS, HD)
            lanes = head_lanes(lse, PLANE * TOK)
            for k in range(PLANE):
                lret[base + k, slot] = lanes[k * TOK:(k + 1) * TOK]

        def go(d):
            out_copy(d, me).start()
            lse_copy(d, me).start()

        peers(j, go)

    pl.loop(0, 1)(serve)
    for dz in range(1, zs):
        kv1(dz, (z + zs - dz) % zs).wait_recv()
    for dy in range(1, ys):
        kv2(dy, y).start()
    pl.loop(1, 2)(serve)
    for dy in range(1, ys):
        kv2(dy, (y + ys - dy) % ys).wait_recv()
    kv3(core).start()
    pl.loop(2, planes)(serve)
    back[me] = ret[me]
    lback[me] = lret[me]
    kv3(1 - core).wait_recv()

    span_f = span[...].astype(jnp.float32)
    mine = jnp.sum(
        jnp.where(lax.broadcasted_iota(jnp.int32, span_f.shape, 1) == me, span_f, 0.0),
        axis=1, keepdims=True)
    order = jnp.clip(span_f - mine, -1.0, 1.0).astype(jnp.bfloat16)
    group = 16
    keys = group * PER_DEV
    zgroup = group // (2 * ys)
    chunks = n // group
    key_lane = lax.broadcasted_iota(jnp.int32, (REQUESTS, keys), 1)
    key_row = lax.broadcasted_iota(jnp.int32, (REQUESTS, keys), 0)

    def ranks(chunk):
        lane = lax.broadcasted_iota(jnp.int32, (n, keys), 1)
        dev = lax.broadcasted_iota(jnp.int32, (n, keys), 0)
        pick = jnp.where(lane // PER_DEV + chunk * group == dev, 1.0, 0.0).astype(jnp.bfloat16)
        step = jnp.dot(order, pick, preferred_element_type=jnp.float32)
        spot_rank = step * TOK + (key_lane % TOK).astype(jnp.float32)
        same = (key_lane // TOK) % REQUESTS == key_row
        return jnp.where(same, spot_rank, 100.0).astype(jnp.bfloat16)

    def kv_rows(chunk, which):
        if chunks == 1:
            return kv[:, :, :, which].reshape(keys, HD)
        flat = kv.at[:, :, :, which]
        per_z = (2 * ys) // group
        if per_z:
            got = flat[chunk // per_z, pl.ds((chunk % per_z) * (group // 2), group // 2)]
        else:
            got = flat[pl.ds(chunk * zgroup, zgroup)]
        return got.reshape(keys, HD)

    def prompt_part(c, chunk, rank):
        q = qx_rows(c)
        row = lax.broadcasted_iota(jnp.int32, (ROWS, REQUESTS), 0)
        req = lax.broadcasted_iota(jnp.int32, (ROWS, REQUESTS), 1)
        spread = jnp.where(row // (TOK * HEADS) + c * (ROWS // (TOK * HEADS)) == req, 1.0, 0.0)
        ranked = jnp.dot(spread.astype(jnp.bfloat16), rank, preferred_element_type=jnp.float32)
        token = (lax.broadcasted_iota(jnp.int32, (ROWS, 1), 0) // HEADS) % TOK
        return attend(q, kv_rows(chunk, 0), kv_rows(chunk, 1), ranked <= token.astype(jnp.float32))

    reqs = ROWS // (TOK * HEADS)

    def qx_rows(c):
        return qx[pl.ds(c * reqs, reqs)].reshape(ROWS, HD)

    rank0 = ranks(0) if chunks == 1 else None

    @pl.loop(0, REQUESTS // reqs)
    def _(c):
        if chunks == 1:
            m, o = prompt_part(c, 0, rank0)
        else:
            def more(chunk, carry):
                m0, o0 = carry
                m1, o1 = prompt_part(c, chunk, ranks(chunk))
                m2 = jnp.maximum(m0, m1)
                return m2, (o0 * jnp.exp2((m0 - m2) * EXP2_SCALE)
                            + o1 * jnp.exp2((m1 - m2) * EXP2_SCALE))
            m, o = lax.fori_loop(0, chunks, more, (
                jnp.full((ROWS, 1), FLOOR, jnp.float32), jnp.zeros((ROWS, 2 * HD), jnp.float32)))
        total = o[:, HD:]
        pout[pl.ds(c * reqs, reqs)] = (o[:, :HD] / total).reshape(reqs, TOK, HEADS, HD)
        lanes = head_lanes(m * EXP2_SCALE + jnp.log2(total), reqs * TOK)
        plse[pl.ds(pl.multiple_of(c * reqs * TOK, reqs * TOK), reqs * TOK)] = lanes

    def finish(d):
        out_copy(d, d).wait_recv()
        lse_copy(d, d).wait_recv()

    pl.loop(0, planes)(lambda j: peers(j, finish))

    for i in range(hit_count):
        for r in range(REQUESTS):
            owner = hits[r, i]
            rank = jnp.int32(0)
            for r2 in range(r):
                for i2 in range(hit_count):
                    rank = jnp.where(hits[r2, i2] == owner, rank + 1, rank)
            rank = jnp.minimum(rank, CAP - 1)
            comb[i, r] = back[owner, rank]
            lcomb[i, r * TOK:(r + 1) * TOK] = lback[owner, rank]

    top = plse[...]
    for i in range(hit_count):
        top = jnp.maximum(top, lcomb[i])
    share = jnp.exp2(plse[...] - top)
    shares = [jnp.exp2(lcomb[i] - top) for i in range(hit_count)]
    scale = 1.0 / functools.reduce(jnp.add, shares, share)
    whole = (PER_DEV, HEADS, HD)
    mixed = head_rows(share * scale, PER_DEV) * pout[...].reshape(whole)
    for i in range(hit_count):
        mixed = mixed + head_rows(shares[i] * scale, PER_DEV) * comb[i].reshape(whole).astype(jnp.float32)
    out[...] = mixed.astype(jnp.bfloat16)

    def drained(d):
        query_copy(d, me).wait_send()
        out_copy(d, me).wait_send()
        lse_copy(d, me).wait_send()

    pl.loop(0, planes)(lambda j: peers(j, drained))
    for dz in range(1, zs):
        kv1(dz, z).wait_send()
    for dy in range(1, ys):
        kv2(dy, y).wait_send()
    kv3(core).wait_send()


def solution(mesh):
    n = mesh.shape["cache"]
    rest = n // 2
    zs = 2 ** ((int(math.log2(rest)) + 1) // 2)
    dims = (zs, rest // zs)

    def body(prefix_len, hits, span_block, queries, fresh_keys, fresh_values, cache_keys, cache_values):
        hit_count = hits.shape[1]
        units = queries.reshape(REQUESTS, TOK, HEADS, HD)
        vmem = pl.BlockSpec(memory_space=pltpu.VMEM)
        smem = pl.BlockSpec(memory_space=pltpu.SMEM)
        hbm = pl.BlockSpec(memory_space=pltpu.HBM)
        bf16, f32 = jnp.bfloat16, jnp.float32
        dma = pltpu.SemaphoreType.DMA
        block = (n, CAP, TOK, HEADS, HD)
        result = pl.pallas_call(
            functools.partial(kernel, n, hit_count, dims),
            out_shape=jax.ShapeDtypeStruct((PER_DEV, HEADS, HD), bf16),
            in_specs=[smem, smem, vmem, vmem, hbm, hbm, hbm, hbm],
            out_specs=vmem,
            scratch_shapes=[
                pltpu.VMEM(block, bf16), pltpu.VMEM(block, bf16),
                pltpu.VMEM(block, bf16), pltpu.VMEM(block, bf16),
                pltpu.VMEM((n, CAP, TOK, HD), f32), pltpu.VMEM((n, CAP, TOK, HD), f32),
                pltpu.VMEM(dims + (2, 2, PER_DEV, HD), bf16),
                pltpu.VMEM((CAP * REGION, HD), bf16), pltpu.VMEM((CAP * REGION, HD), bf16),
                pltpu.VMEM((REQUESTS, TOK, HEADS, HD), f32), pltpu.VMEM((PER_DEV, HD), f32),
                pltpu.VMEM((hit_count, REQUESTS, TOK, HEADS, HD), bf16),
                pltpu.VMEM((hit_count, PER_DEV, HD), f32),
            ] + [dma((n,))] * 6 + [dma((dims[0],))] * 2 + [dma((dims[1],))] * 2 + [dma((1,))] * 2 + [dma((4,))],
            compiler_params=pltpu.CompilerParams(
                collective_id=0, has_side_effects=True, vmem_limit_bytes=48 << 20),
        )(prefix_len, hits, span_block, units, fresh_keys, fresh_values, cache_keys, cache_values)
        return result.reshape(PER_DEV, HEADS * HD)

    in_specs = (
        P("groups"), P("groups", None), P("groups", None),
        P(("groups", "cache"), None), P(("groups", "cache"), None), P(("groups", "cache"), None),
        P(("groups", "cache"), None), P(("groups", "cache"), None),
    )
    return jax.shard_map(body, mesh=mesh, in_specs=in_specs,
                         out_specs=P(("groups", "cache"), None), check_vma=False)
```

```python
import functools
import math

import jax
import jax.numpy as jnp
from jax import lax
from jax.experimental import pallas as pl
from jax.experimental.pallas import tpu as pltpu
from jax.sharding import PartitionSpec as P

HEADS = 16
HD = 128
PAGE = 128
CAP = 2
REQUESTS = 16
TOK = 4
PAGES_DEV = 16
REGION = PAGES_DEV // CAP * PAGE
PER_DEV = REQUESTS * TOK
PLANE = 4
ROWS = PLANE * TOK * HEADS
MESH = pl.DeviceIdType.MESH
FLOOR = -1e30
EXP2_SCALE = HD**-0.5 * math.log2(math.e)


def flip(a, b, size):
    out, bit = 0, 1
    while bit < size:
        out = out + ((a // bit + b // bit) % 2) * bit
        bit *= 2
    return out


def attend(q, k, v, visible):
    s = lax.dot_general(q, k, (((1,), (1,)), ((), ())), preferred_element_type=jnp.float32)
    s = jnp.where(visible, s, FLOOR)
    m = jnp.max(s, axis=1, keepdims=True)
    p = jnp.exp2((s - m) * EXP2_SCALE).astype(jnp.bfloat16)
    v1 = jnp.concatenate([v, jnp.ones_like(v)], axis=1)
    o = jnp.dot(p, v1, preferred_element_type=jnp.float32)
    return m, o


def head_lanes(x, units, first):
    row = lax.broadcasted_iota(jnp.int32, (units, TOK * HEADS, HD), 1)
    lane = lax.broadcasted_iota(jnp.int32, (units, TOK * HEADS, HD), 2)
    wide = x.reshape(units, TOK * HEADS, HD)
    return jnp.sum(jnp.where(row + first == lane, wide, 0.0), axis=1)


def head_rows(x, units):
    row = lax.broadcasted_iota(jnp.int32, (units, TOK * HEADS, HD), 1)
    lane = lax.broadcasted_iota(jnp.int32, (units, TOK * HEADS, HD), 2)
    wide = jnp.broadcast_to(x[:, None, :], (units, TOK * HEADS, HD))
    return jnp.sum(jnp.where(row == lane, wide, 0.0), axis=2, keepdims=True)


def mirrored(a, size):
    out, bit = 0, 1
    while bit < size:
        out = out + ((a // bit) % 2) * (size // (2 * bit))
        bit *= 2
    return out


def kernel(n, hit_count, prefix, hits, span, queries, fk, fv, ck, cv, out,
           qin, qx, send, arrived, ret, back, lret, lback, kv, kc, vc, pout, plse, comb, lcomb,
           qs, qr, rs, rr, ls, lr, s1s, s1r, loc):
    me = lax.axis_index("cache")
    planes = n // PLANE
    stages = int(math.log2(n))
    spot_me = mirrored(me, n)
    my_plane = me // PLANE

    loads = [
        pltpu.make_async_copy(queries, qin, loc.at[4]),
        pltpu.make_async_copy(fk, kv.at[spot_me, 0], loc.at[0]),
        pltpu.make_async_copy(fv, kv.at[spot_me, 1], loc.at[1]),
        pltpu.make_async_copy(ck, kc, loc.at[2]),
        pltpu.make_async_copy(cv, vc, loc.at[3]),
    ]
    for load in loads:
        load.start()

    barrier = pltpu.get_barrier_semaphore()

    @pl.loop(1, n)
    def _(k):
        pl.semaphore_signal(barrier, inc=1, device_id={"cache": (me + k) % n}, device_id_type=MESH)

    def named_by(d):
        first = jnp.int32(REQUESTS - 1)
        last = jnp.int32(0)
        for r in range(REQUESTS):
            for i in range(hit_count):
                here = hits[r * hit_count + i] == d
                first = jnp.where(here, jnp.minimum(first, r), first)
                last = jnp.where(here, r, last)
        return first, last

    loads[0].wait()
    qx[...] = qin[...].reshape(REQUESTS, TOK, HEADS, HD)

    @pl.loop(0, n)
    def _(d):
        first, last = named_by(d)
        send[d, 0] = qx[first]
        send[d, 1] = qx[last]

    pl.semaphore_wait(barrier, n - 1)
    loads[1].wait()
    loads[2].wait()

    def kv_copy(t, mine=True):
        size = 2**t
        start = (spot_me // size) * size
        if not mine:
            start = flip(spot_me // size, 1, n // size) * size
        block = kv.at[pl.ds(start, size)]
        return pltpu.make_async_remote_copy(
            src_ref=block, dst_ref=block, send_sem=s1s.at[t], recv_sem=s1r.at[t],
            device_id={"cache": flip(me, n // (2 * size), n)}, device_id_type=MESH)

    kv_copy(0).start()

    def query_copy(to, frm):
        return pltpu.make_async_remote_copy(
            src_ref=send.at[to], dst_ref=arrived.at[frm], send_sem=qs.at[to], recv_sem=qr.at[frm],
            device_id={"cache": to}, device_id_type=MESH)

    def out_copy(to, frm):
        return pltpu.make_async_remote_copy(
            src_ref=ret.at[to], dst_ref=back.at[frm], send_sem=rs.at[to], recv_sem=rr.at[frm],
            device_id={"cache": to}, device_id_type=MESH)

    def lse_copy(to, frm):
        return pltpu.make_async_remote_copy(
            src_ref=lret.at[to], dst_ref=lback.at[frm], send_sem=ls.at[to], recv_sem=lr.at[frm],
            device_id={"cache": to}, device_id_type=MESH)

    def peers(j, act):
        base = flip(my_plane, j, planes) * PLANE

        @pl.loop(0, PLANE)
        def _(k):
            d = base + (me + k) % PLANE

            @pl.when(d != me)
            def _():
                act(d)

    @pl.loop(0, planes)
    def _(i):
        peers(i, lambda d: query_copy(d, me).start())

    arrived[me] = send[me]
    loads[3].wait()
    loads[4].wait()

    limits = []
    for request in named_by(me):
        place = jnp.int32(0)
        for i in range(hit_count):
            place = jnp.where(hits[request * hit_count + i] == me, i, place)
        limits.append(prefix[request] - place * REGION)
    spot = lax.broadcasted_iota(jnp.int32, (1, REGION), 1)

    def serve(j):
        peers(j, lambda d: query_copy(d, d).wait_recv())
        base = flip(my_plane, j, planes) * PLANE
        lanes = jnp.zeros((PLANE, HD), jnp.float32)

        for slot in range(CAP):
            q = arrived[pl.ds(base, PLANE), slot].reshape(ROWS, HD)
            part = pl.ds(slot * REGION, REGION)
            m, o = attend(q, kc[part], vc[part], spot < limits[slot])
            total = jnp.maximum(o[:, HD:], 1.0)
            lse = m * EXP2_SCALE + jnp.log2(total)
            lse = jnp.where(limits[slot] > 0, lse, FLOOR)
            result = (o[:, :HD] / total).astype(jnp.bfloat16)
            ret[pl.ds(base, PLANE), slot] = result.reshape(PLANE, TOK, HEADS, HD)
            lanes = lanes + head_lanes(lse, PLANE, slot * TOK * HEADS)
        for k in range(PLANE):
            lret[base + k] = lanes[k:k + 1]

        def go(d):
            out_copy(d, me).start()
            lse_copy(d, me).start()

        peers(j, go)

        for t in range(stages - 1):
            @pl.when(j == t)
            def _():
                kv_copy(t, mine=False).wait_recv()
                kv_copy(t + 1).start()

    pl.loop(0, planes)(serve)
    back[me] = ret[me]
    lback[me] = lret[me]
    kv_copy(stages - 1, mine=False).wait_recv()

    span_f = span[...].astype(jnp.float32)
    mine = jnp.sum(
        jnp.where(lax.broadcasted_iota(jnp.int32, span_f.shape, 1) == me, span_f, 0.0),
        axis=1, keepdims=True)
    order = jnp.clip(span_f - mine, -1.0, 1.0).astype(jnp.bfloat16)
    group = 16
    keys = group * PER_DEV
    chunks = n // group
    key_lane = lax.broadcasted_iota(jnp.int32, (REQUESTS, keys), 1)
    key_row = lax.broadcasted_iota(jnp.int32, (REQUESTS, keys), 0)

    def ranks(chunk):
        lane = lax.broadcasted_iota(jnp.int32, (n, keys), 1)
        dev = lax.broadcasted_iota(jnp.int32, (n, keys), 0)
        pick = jnp.where(mirrored(lane // PER_DEV + chunk * group, n) == dev, 1.0, 0.0).astype(jnp.bfloat16)
        step = jnp.dot(order, pick, preferred_element_type=jnp.float32)
        spot_rank = step * TOK + (key_lane % TOK).astype(jnp.float32)
        same = (key_lane // TOK) % REQUESTS == key_row
        return jnp.where(same, spot_rank, 100.0).astype(jnp.bfloat16)

    def kv_rows(chunk, which):
        return kv[pl.ds(chunk * group, group), which].reshape(keys, HD)

    def prompt_part(c, chunk, rank):
        q = qx_rows(c)
        row = lax.broadcasted_iota(jnp.int32, (ROWS, REQUESTS), 0)
        req = lax.broadcasted_iota(jnp.int32, (ROWS, REQUESTS), 1)
        spread = jnp.where(row // (TOK * HEADS) + c * (ROWS // (TOK * HEADS)) == req, 1.0, 0.0)
        ranked = jnp.dot(spread.astype(jnp.bfloat16), rank, preferred_element_type=jnp.float32)
        token = (lax.broadcasted_iota(jnp.int32, (ROWS, 1), 0) // HEADS) % TOK
        return attend(q, kv_rows(chunk, 0), kv_rows(chunk, 1), ranked <= token.astype(jnp.float32))

    reqs = ROWS // (TOK * HEADS)

    def qx_rows(c):
        return qx[pl.ds(c * reqs, reqs)].reshape(ROWS, HD)

    rank0 = ranks(0) if chunks == 1 else None

    @pl.loop(0, REQUESTS // reqs)
    def _(c):
        if chunks == 1:
            m, o = prompt_part(c, 0, rank0)
        else:
            def more(chunk, carry):
                m0, o0 = carry
                m1, o1 = prompt_part(c, chunk, ranks(chunk))
                m2 = jnp.maximum(m0, m1)
                return m2, (o0 * jnp.exp2((m0 - m2) * EXP2_SCALE)
                            + o1 * jnp.exp2((m1 - m2) * EXP2_SCALE))
            m, o = lax.fori_loop(0, chunks, more, (
                jnp.full((ROWS, 1), FLOOR, jnp.float32), jnp.zeros((ROWS, 2 * HD), jnp.float32)))
        total = o[:, HD:]
        pout[pl.ds(c * reqs, reqs)] = (o[:, :HD] / total).reshape(reqs, TOK, HEADS, HD)
        plse[pl.ds(pl.multiple_of(c * reqs, reqs), reqs)] = head_lanes(m * EXP2_SCALE + jnp.log2(total), reqs, 0)

    def finish(d):
        out_copy(d, d).wait_recv()
        lse_copy(d, d).wait_recv()

    pl.loop(0, planes)(lambda j: peers(j, finish))

    for i in range(hit_count):
        for r in range(REQUESTS):
            owner = hits[r * hit_count + i]
            rank = jnp.int32(0)
            for r2 in range(r):
                for i2 in range(hit_count):
                    rank = jnp.where(hits[r2 * hit_count + i2] == owner, rank + 1, rank)
            rank = jnp.minimum(rank, CAP - 1)
            comb[i, r] = back[owner, rank]
            row = lback[owner]
            lcomb[i, r:r + 1] = jnp.where(rank == 0, row, pltpu.roll(row, HD // 2, 1))

    top = plse[...]
    for i in range(hit_count):
        top = jnp.maximum(top, lcomb[i])
    share = jnp.exp2(plse[...] - top)
    shares = [jnp.exp2(lcomb[i] - top) for i in range(hit_count)]
    scale = 1.0 / functools.reduce(jnp.add, shares, share)
    whole = (REQUESTS, TOK * HEADS, HD)
    mixed = head_rows(share * scale, REQUESTS) * pout[...].reshape(whole)
    for i in range(hit_count):
        mixed = mixed + head_rows(shares[i] * scale, REQUESTS) * comb[i].reshape(whole).astype(jnp.float32)
    out[...] = mixed.astype(jnp.bfloat16).reshape(PER_DEV, HEADS, HD)

    def drained(d):
        query_copy(d, me).wait_send()
        out_copy(d, me).wait_send()
        lse_copy(d, me).wait_send()

    pl.loop(0, planes)(lambda j: peers(j, drained))
    for t in range(stages):
        kv_copy(t).wait_send()


def solution(mesh):
    n = mesh.shape["cache"]

    def body(prefix_len, hits, span_block, queries, fresh_keys, fresh_values, cache_keys, cache_values):
        hit_count = hits.shape[1]
        vmem = pl.BlockSpec(memory_space=pltpu.VMEM)
        smem = pl.BlockSpec(memory_space=pltpu.SMEM)
        hbm = pl.BlockSpec(memory_space=pltpu.HBM)
        bf16, f32 = jnp.bfloat16, jnp.float32
        dma = pltpu.SemaphoreType.DMA
        block = (n, CAP, TOK, HEADS, HD)
        result = pl.pallas_call(
            functools.partial(kernel, n, hit_count),
            out_shape=jax.ShapeDtypeStruct((PER_DEV, HEADS, HD), bf16),
            in_specs=[smem, smem, vmem, hbm, hbm, hbm, hbm, hbm],
            out_specs=vmem,
            scratch_shapes=[
                pltpu.VMEM((PER_DEV, HEADS * HD), bf16), pltpu.VMEM((REQUESTS, TOK, HEADS, HD), bf16),
                pltpu.VMEM(block, bf16), pltpu.VMEM(block, bf16),
                pltpu.VMEM(block, bf16), pltpu.VMEM(block, bf16),
                pltpu.VMEM((n, 1, HD), f32), pltpu.VMEM((n, 1, HD), f32),
                pltpu.VMEM((n, 2, PER_DEV, HD), bf16),
                pltpu.VMEM((CAP * REGION, HD), bf16), pltpu.VMEM((CAP * REGION, HD), bf16),
                pltpu.VMEM((REQUESTS, TOK, HEADS, HD), f32), pltpu.VMEM((REQUESTS, HD), f32),
                pltpu.VMEM((hit_count, REQUESTS, TOK, HEADS, HD), bf16),
                pltpu.VMEM((hit_count, REQUESTS, HD), f32),
            ] + [dma((n,))] * 6 + [dma((int(math.log2(n)),))] * 2 + [dma((5,))],
            compiler_params=pltpu.CompilerParams(
                collective_id=0, has_side_effects=True, vmem_limit_bytes=60 << 20),
        )(prefix_len, hits.reshape(-1), span_block, queries, fresh_keys, fresh_values, cache_keys, cache_values)
        return result.reshape(PER_DEV, HEADS * HD)

    in_specs = (
        P("groups"), P("groups", None), P("groups", None),
        P(("groups", "cache"), None), P(("groups", "cache"), None), P(("groups", "cache"), None),
        P(("groups", "cache"), None), P(("groups", "cache"), None),
    )
    return jax.shard_map(body, mesh=mesh, in_specs=in_specs,
                         out_specs=P(("groups", "cache"), None), check_vma=False)
```
